512 devices in a mesh: quad: 16 (over z), slab: 32 (over y, x, core).
Axes of the slice: x: 4, y: 4, z: 16, core: 2. Of those that a mesh axis runs over, the one named last changes fastest.
Arguments:
- factors: bfloat16 [16, 32, 2, 512, 512], P('quad', 'slab'), may hold values from -0.1875 to 0.1875
- onsite: float32 [32, 512, 512], P('slab'), may hold values from -0.25 to 0.25, as said below
- coupling: float32 [32, 128, 128], P('slab'), may hold values from -1 to 1
- vectors: bfloat16 [32, 512, 128], P('slab'), may hold values from -1.5 to 1.5
- quad_weight: float32 [16, 2], P('quad'), may hold values from -0.6 to 0.6
Outputs:
- subspace: float32 [32, 512, 128], P('slab', 'quad')
- correlation: float32 [128, 128], replicated
- projected: float32 [128, 128], replicated
The draws below stay inside these ranges and needn't reach their ends.
Inputs may be any that keep to these rules, and one draw needn't show every extreme that they name: `onsite`: each diagonal block is symmetric, and its largest entry magnitude is exactly 8 / sqrt(1024).
All inputs are finite; a program needn't handle non-finite values.
Results may differ from the reference program's by a relative error of at most 0.0003.
Values sent between devices are 32-bit elements; how exact they have to be, the bound alone decides.
No kernel may reach another device: no remote copies, remote signals or barrier semaphores. Data moves between devices by JAX's collectives and lax.ppermute only.
A program may use at most 64 MiB of HBM per device.

```python
import jax
import jax.numpy as jnp
from jax import lax

B = 512
M = 128
R = 128
NQ = 16
NSLABS = 32


def draw_onsite(key, part):
    normal_draw = jax.random.normal(key, (NSLABS, B, B), jnp.float32)
    clipped = jnp.clip(normal_draw, -4.0, 4.0)
    summed = clipped + jnp.swapaxes(clipped, 1, 2)
    largest = jnp.max(jnp.abs(summed), axis=(1, 2), keepdims=True)
    return summed / largest * (8.0 / jnp.sqrt(2.0 * B))


def shard_levels(rng, extent, split, least, high):
    loudness, own = 1.0, jax.random.fold_in(rng, 6)
    for axis_at, parts in split:
        steps = jnp.exp(jax.random.uniform(jax.random.fold_in(own, axis_at), (parts,), jnp.float32, least / len(split), high / len(split)))
        loudness = loudness * jnp.repeat(steps, extent[axis_at] // parts).reshape([-1 if axis == axis_at else 1 for axis in range(len(extent))])
    return loudness


def gaussian(stream_key, shape, scale, limit, cuts=(), held_as=jnp.bfloat16):
    loudness = shard_levels(stream_key, shape, cuts, -0.22, 0.18) if cuts else 1.0
    values = jax.random.normal(stream_key, shape, jnp.float32) * scale * loudness
    return jnp.minimum(jnp.maximum(values, -limit), limit).astype(held_as)


def setup_inputs(seed: int = 0) -> dict:
    keys = jax.random.split(jax.random.key(seed), 6)
    factors = gaussian(keys[0], (NQ, NSLABS, 2, B, B), (2 * B) ** -0.5, 0.1875, ((0, 16), (1, 32)))
    onsite = draw_onsite(jax.random.fold_in(keys[5], 71), 0)
    coupling = gaussian(keys[2], (NSLABS, R, R), (4 * R // 15) ** -0.5, 1.0, ((0, 32),), jnp.float32)
    vectors = gaussian(keys[3], (NSLABS, B, M), 0.25, 1.5, ((0, 32),))
    quad_weight = gaussian(keys[4], (NQ, 2), 0.1, 0.6, ((0, 16),), jnp.float32)
    return dict(factors=factors, onsite=onsite, coupling=coupling, vectors=vectors, quad_weight=quad_weight)


precise = lax.Precision.HIGHEST


def complex_times(left_cols, right_cols):
    real_part = jnp.dot(left_cols[0], right_cols[0], precision=precise, preferred_element_type=jnp.float32) - jnp.dot(left_cols[1], right_cols[1], precision=precise, preferred_element_type=jnp.float32)
    imag_part = jnp.dot(left_cols[0], right_cols[1], precision=precise, preferred_element_type=jnp.float32) + jnp.dot(left_cols[1], right_cols[0], precision=precise, preferred_element_type=jnp.float32)
    return jnp.stack([real_part, imag_part])


def real_times(real_left, right_cols):
    return jnp.stack([jnp.dot(real_left, right_cols[0], precision=precise, preferred_element_type=jnp.float32), jnp.dot(real_left, right_cols[1], precision=precise, preferred_element_type=jnp.float32)])


def reference(factors, onsite, coupling, vectors, quad_weight):
    zero_state = jnp.zeros((2, R, M), jnp.float32)

    def one_point(running, inputs):
        blocks, weight = inputs

        def forward_step(incoming, pieces):
            factor_block, vector_block, link_block = pieces
            source = jnp.dot(factor_block.reshape(2 * B, B), vector_block, preferred_element_type=jnp.float32).reshape(2, B, M)
            left_cols = factor_block[:, :, :R].astype(jnp.float32)
            solved = source + complex_times(left_cols, incoming)
            handed = real_times(link_block.T, solved[:, B - R:])
            return handed, solved

        unused, partial_rows = lax.scan(forward_step, zero_state, (blocks, vectors, coupling))

        def backward_step(incoming, pieces):
            factor_block, solved, link_block = pieces
            right_cols = factor_block[:, :, B - R:].astype(jnp.float32)
            result = solved + complex_times(right_cols, real_times(link_block, incoming))
            return result[:, :R], weight[0] * result[0] - weight[1] * result[1]

        unused, filtered = lax.scan(backward_step, zero_state, (blocks, partial_rows, coupling), reverse=True)
        return running + filtered, None

    subspace, unused = lax.scan(one_point, jnp.zeros((NSLABS, B, M), jnp.float32), (factors, quad_weight))
    diagonal_part = jnp.einsum("sbk,skm->sbm", onsite, subspace, precision=precise)
    next_planes = jnp.concatenate([subspace[1:, :R], jnp.zeros((1, R, M), jnp.float32)], axis=0)
    upper_part = jnp.einsum("sab,sbm->sam", coupling, next_planes, precision=precise)
    prev_planes = jnp.concatenate([jnp.zeros((1, R, M), jnp.float32), subspace[:-1, B - R:]], axis=0)
    prev_links = jnp.concatenate([jnp.zeros((1, R, R), jnp.float32), coupling[:-1]], axis=0)
    lower_part = jnp.einsum("sba,sbm->sam", prev_links, prev_planes, precision=precise)
    applied = jnp.concatenate([diagonal_part[:, :R] + lower_part, diagonal_part[:, R:B - R], diagonal_part[:, B - R:] + upper_part], axis=1)
    flattened = subspace.reshape(NSLABS * B, M)
    rows_all = NSLABS * B
    correlation = jnp.dot(flattened.T, flattened, precision=precise, preferred_element_type=jnp.float32) / rows_all
    projected = jnp.dot(flattened.T, applied.reshape(NSLABS * B, M), precision=precise, preferred_element_type=jnp.float32) / rows_all
    return (subspace, correlation, projected)
```

```python
import functools

import jax
import jax.numpy as jnp
from jax import lax
from jax.experimental import pallas as pl
from jax.experimental.pallas import tpu as pltpu
from jax.sharding import Mesh
from jax.sharding import PartitionSpec as P

F32 = jnp.float32
BF16 = jnp.bfloat16
SLAB = ("y1", "y0", "x1", "x0", "core")
VMEM_BYTES = 24 << 20


def split(x):
    high = x.astype(BF16)
    return high, (x - high.astype(F32)).astype(BF16)


def dot(a, b):
    return jnp.dot(a, b, preferred_element_type=F32)


def times(left, right):
    return dot(left[0], right[0]) + (dot(left[0], right[1]) + dot(left[1], right[0]))


def wide(real, imag):
    return tuple(
        jnp.concatenate([jnp.concatenate([r, -i], 1), jnp.concatenate([i, r], 1)], 0)
        for r, i in zip(split(real), split(imag))
    )


class Pair:
    def __init__(self, get, rows):
        self.get, self.rows = get, rows

    def block(self, half, which, side):
        n = 2 * self.rows
        return self.get(half, side)[which * n : (which + 1) * n, :]

    def c_part(self, half, side):
        return self.get(half, side)[4 * self.rows : 5 * self.rows, :]

    def wide_block(self, which, side):
        m = self.block(0, which, side)
        return wide(m[: self.rows], m[self.rows :])

    def wide_c(self, side):
        return wide(self.c_part(0, side), self.c_part(1, side))


def merged(pair, half, need_a=True, need_c=True):
    start = split(pair.block(half, 0, 0))
    new_x = new_c = None
    if need_a:
        new_x = times(pair.wide_block(0, 1), start)
        if half:
            new_x = new_x + pair.block(1, 0, 1)
    z = times(pair.wide_block(1, 1), start)
    if half:
        z = z + pair.block(1, 1, 1)
    turn = pair.wide_c(0)
    new_w = pair.block(half, 1, 0) + times(turn, split(z))
    if need_c:
        rows = slice(half * pair.rows, (half + 1) * pair.rows)
        upper = jnp.concatenate([pair.c_part(0, 1), pair.c_part(1, 1)], 0)
        new_c = times((turn[0][rows], turn[1][rows]), split(upper))
    return new_x, new_w, new_c


def gathered_pair(own, other, half, rows):
    halves = (own, other) if half == 0 else (other, own)
    return Pair(lambda h, side: halves[h].at[side], rows)


def leaf_pair(own, other, half, rows):
    sides = (own, other) if half == 0 else (other, own)
    return Pair(lambda h, side: sides[side].at[h], rows)


def leaf_kernel(factor, link, vectors, out):
    rows = link.shape[0]
    last = factor.shape[1] - rows
    v, v_t = split(link[...]), split(link[...].T)
    y = vectors[...]
    for part in (0, 1):
        low, high = factor[part, :rows, :], factor[part, last:, :]
        at = slice(part * rows, (part + 1) * rows)
        left = high[:, :rows]
        out[0, at, :] = dot(v_t[0], left) + dot(v_t[1], left)
        out[1, at, :] = times(v_t, split(dot(high, y)))
        at = slice((2 + part) * rows, (3 + part) * rows)
        out[0, at, :] = low[:, :rows].astype(F32)
        out[1, at, :] = dot(low, y)
        right = low[:, last:]
        out[part, 4 * rows :, :] = dot(right, v[0]) + dot(right, v[1])


def merge_kernel(make, place, own, other, out):
    rows = out.shape[0] // 5
    for half in (0, 1):

        @pl.when(place[0] == half)
        def _():
            new_x, new_w, new_c = merged(make(own, other, half, rows), half)
            out[: 2 * rows, :] = new_x
            out[2 * rows : 4 * rows, :] = new_w
            out[4 * rows :, :] = new_c


def top_kernel(place, own, other, out):
    rows = out.shape[0] // 2

    @pl.when(place[0] == 0)
    def _():
        out[...] = merged(gathered_pair(own, other, 0, rows), 0, False, False)[1]

    @pl.when(place[0] == 1)
    def _():
        new_b, new_c, unused = merged(gathered_pair(own, other, 1, rows), 1, True, False)
        out[...] = jnp.where(place[4] == 0, new_b, new_c)


def down_kernel(place, weight, factor, link, vectors, top, *refs):
    *levels, out = refs
    rows, columns = link.shape
    orbitals = factor.shape[1]
    zero = jnp.zeros((2 * rows, columns), F32)

    def sweep(half):
        b_low, d_up, c_up = top[1, 0], top[0, 1], top[1, 1]
        mid = c_up + times(wide(d_up[:rows], d_up[rows:]), split(b_low))
        upper = place[4] == 1
        u, t = jnp.where(upper, b_low, zero), jnp.where(upper, zero, mid)
        for depth, make in ((3, gathered_pair), (2, gathered_pair), (1, gathered_pair), (0, leaf_pair)):
            own, other = levels[2 * depth], levels[2 * depth + 1]
            pair = make(own, other, half, rows)
            u_mid = times(pair.wide_block(0, 0), split(u)) + pair.block(1, 0, 0)
            t_mid = pair.block(1, 1, 1) + times(pair.wide_c(1), split(t))
            t_mid = t_mid + times(pair.wide_block(1, 1), split(u_mid))
            if depth == 0:
                u, t = (u, t_mid) if half == 0 else (u_mid, t)
            else:
                upper = place[depth] == 1
                u, t = jnp.where(upper, u_mid, u), jnp.where(upper, t, t_mid)
        w_re, w_im = weight[0, 0], weight[0, 1]
        turned = (w_re * u[:rows] - w_im * u[rows:], w_re * u[rows:] + w_im * u[:rows])
        after = (w_re * t[:rows] - w_im * t[rows:], w_re * t[rows:] + w_im * t[:rows])
        v = split(link[...])
        y = vectors[...].astype(F32)
        total = None
        for part, w in ((0, w_re), (1, -w_im)):
            sign = 1.0 if part == 0 else -1.0
            field = w * y
            moved = times(v, split(after[part]))
            field = jnp.concatenate(
                [
                    field[:rows] + sign * turned[part],
                    field[rows : orbitals - rows],
                    field[orbitals - rows :] + sign * moved,
                ],
                0,
            )
            high, low = split(field)
            f = factor[part]
            term = dot(f, high) + dot(f, low)
            total = term if total is None else total + term
        count = out.shape[0]
        share, spare = orbitals // count, rows // count
        for q in range(count):
            out[q, :share, :] = total[q * share : (q + 1) * share]
            out[q, share:, :] = after[0][q * spare : (q + 1) * spare]

    for half in (0, 1):

        @pl.when(place[0] == half)
        def _():
            sweep(half)


def tile_kernel(field, onsite, link, out):
    columns = field.shape[2]
    orbitals, rows = onsite.shape[0], link.shape[0]
    share = orbitals // field.shape[0]
    whole = field[:, :share, :].reshape(orbitals, columns)
    following = field[:, share:, :].reshape(rows, columns)
    parts = split(whole)
    weighted = 0.5 * times(split(onsite[...]), parts)
    coupled = times(split(link[...]), split(following))
    weighted = jnp.concatenate([weighted[: orbitals - rows], weighted[orbitals - rows :] + coupled], 0)
    flipped = tuple(p.T for p in parts)
    gram = times(flipped, parts)
    tile = times(flipped, split(weighted))
    tile = tile + tile.T
    row = lax.broadcasted_iota(jnp.int32, gram.shape, 0)
    col = lax.broadcasted_iota(jnp.int32, gram.shape, 1)
    packed = jnp.where(row <= col, gram, tile)
    middle = jnp.sum(jnp.where(row == col, tile, 0.0), 0, keepdims=True)
    half = columns // 2
    for h in (0, 1):
        out[h, :half, :] = packed[h * half : (h + 1) * half]
        out[h, half:, :] = jnp.broadcast_to(middle, (8, columns))


def final_kernel(scale, halves, gram_out, tile_out):
    columns = gram_out.shape[1]
    half = columns // 2
    packed = jnp.concatenate([halves[0, :half, :], halves[1, :half, :]], 0) * scale
    middle = jnp.broadcast_to(halves[0, half : half + 1, :] * scale, packed.shape)
    flipped = packed.T
    row = lax.broadcasted_iota(jnp.int32, packed.shape, 0)
    col = lax.broadcasted_iota(jnp.int32, packed.shape, 1)
    gram_out[...] = jnp.where(row <= col, packed, flipped)
    tile_out[...] = jnp.where(row == col, middle, jnp.where(row > col, packed, flipped))


SMEM = pl.BlockSpec(memory_space=pltpu.SMEM)
VMEM = pl.BlockSpec(memory_space=pltpu.VMEM)


def call(kernel, shapes, specs, *args, flops=1 << 26):
    shapes = [jax.ShapeDtypeStruct(s, F32) for s in shapes]
    single = len(shapes) == 1
    return pl.pallas_call(
        kernel,
        out_shape=shapes[0] if single else shapes,
        in_specs=specs,
        out_specs=VMEM if single else [VMEM] * len(shapes),
        compiler_params=pltpu.CompilerParams(vmem_limit_bytes=VMEM_BYTES),
        cost_estimate=pl.CostEstimate(flops=flops, bytes_accessed=1 << 20, transcendentals=0),
    )(*args)


def swapped(x):
    return lax.ppermute(x, "core", [(0, 1), (1, 0)])


def per_device(factors, onsite, coupling, vectors, quad_weight):
    factor, link, here = factors[0, 0], coupling[0], vectors[0]
    orbitals, columns = here.shape
    rows = link.shape[0]
    quads = lax.axis_size("quad")
    place = jnp.stack([lax.axis_index(a) for a in ("core", "x0", "x1", "y0", "y1")]).astype(jnp.int32)
    half_map = (5 * rows, columns)

    leaf = call(leaf_kernel, [(2, *half_map)], [VMEM] * 3, factor, link, here)
    partner = swapped(leaf)
    levels = [leaf, partner]
    mine = call(
        functools.partial(merge_kernel, leaf_pair), [half_map], [SMEM, VMEM, VMEM], place, leaf, partner
    )
    for axis in ("x0", "x1", "y0"):
        own = lax.all_gather(mine, axis)
        other = swapped(own)
        levels += [own, other]
        if axis != "y0":
            mine = call(
                functools.partial(merge_kernel, gathered_pair),
                [half_map],
                [SMEM, VMEM, VMEM],
                place,
                own,
                other,
            )
    mine = call(top_kernel, [(2 * rows, columns)], [SMEM, VMEM, VMEM], place, *levels[-2:])
    top = lax.all_gather(lax.all_gather(mine, "y1"), "core")

    share = orbitals // quads + rows // quads
    terms = call(
        down_kernel,
        [(quads, share, columns)],
        [SMEM, SMEM] + [VMEM] * (4 + len(levels)),
        place,
        quad_weight,
        factor,
        link,
        here,
        top,
        *levels,
    )
    summed = jnp.sum(lax.all_to_all(terms, "quad", 0, 0, tiled=True), axis=0)
    subspace = summed[: orbitals // quads]
    field = lax.all_to_all(
        jnp.broadcast_to(summed[None], (quads, *summed.shape)), "quad", 0, 0, tiled=True
    )
    packed = (columns // 2 + 8, columns)
    tiles = call(tile_kernel, [(2, *packed)], [VMEM] * 3, field, onsite[0], link)
    both = lax.all_gather(tiles, "core")
    core = lax.axis_index("core")
    mine = jnp.sum(lax.dynamic_index_in_dim(both, core, 1, keepdims=False), axis=0)
    plane = SLAB[:4]
    count = lax.axis_size(plane)
    spread = lax.all_to_all(jnp.broadcast_to(mine[None], (count, *packed)), plane, 0, 0, tiled=True)
    halves = lax.all_gather(jnp.sum(spread, axis=0), "core")
    scale = 1.0 / (orbitals * lax.axis_size(SLAB))
    correlation, projected = call(
        functools.partial(final_kernel, scale), [(columns, columns)] * 2, [VMEM], halves
    )
    return subspace[None], correlation, projected


def solution(mesh):
    torus = Mesh(mesh.devices.reshape(mesh.shape["quad"], 2, 2, 2, 2, 2), ("quad", *SLAB))
    return jax.shard_map(
        per_device,
        mesh=torus,
        in_specs=(
            P("quad", SLAB, None, None, None),
            P(SLAB, None, None),
            P(SLAB, None, None),
            P(SLAB, None, None),
            P("quad", None),
        ),
        out_specs=(P(SLAB, "quad", None), P(), P()),
        check_vma=False,
    )
```

```python
import functools

import jax
import jax.numpy as jnp
from jax import lax
from jax.experimental import pallas as pl
from jax.experimental.pallas import tpu as pltpu
from jax.sharding import Mesh
from jax.sharding import PartitionSpec as P

F32 = jnp.float32
BF16 = jnp.bfloat16
SLAB = ("y", "x", "core")
VMEM_BYTES = 24 << 20


def split(x):
    high = x.astype(BF16)
    return high, (x - high.astype(F32)).astype(BF16)


def dot(a, b):
    return jnp.dot(a, b, preferred_element_type=F32)


def times(left, right):
    return dot(left[0], right[0]) + (dot(left[0], right[1]) + dot(left[1], right[0]))


def wide(real, imag):
    return tuple(
        jnp.concatenate([jnp.concatenate([r, -i], 1), jnp.concatenate([i, r], 1)], 0)
        for r, i in zip(split(real), split(imag))
    )


class Run:
    def __init__(self, get, count, rows):
        self.get, self.count, self.rows = get, count, rows

    def block(self, half, which, k):
        n = 2 * self.rows
        return self.get(half, k)[which * n : (which + 1) * n, :]

    def c_part(self, half, k):
        return self.get(half, k)[4 * self.rows : 5 * self.rows, :]

    def wide_block(self, which, k):
        m = self.block(0, which, k)
        return wide(m[: self.rows], m[self.rows :])

    def wide_c(self, k):
        return wide(self.c_part(0, k), self.c_part(1, k))


def merged(run, half):
    states = [run.block(half, 0, 0)]
    for k in range(1, run.count):
        state = times(run.wide_block(0, k), split(states[-1]))
        states.append(state + run.block(1, 0, k) if half else state)

    def from_left(k):
        term = times(run.wide_block(1, k), split(states[k - 1]))
        return term + run.block(1, 1, k) if half else term

    last = run.count - 1
    back, turn = from_left(last), jnp.concatenate([run.c_part(0, last), run.c_part(1, last)], 0)
    columns = back.shape[1]
    for k in range(last - 1, 0, -1):
        both = times(run.wide_c(k), split(jnp.concatenate([back, turn], 1)))
        back, turn = both[:, :columns] + from_left(k), both[:, columns:]
    first = run.wide_c(0)
    back = run.block(half, 1, 0) + times(first, split(back))
    rows = slice(half * run.rows, (half + 1) * run.rows)
    return states[-1], back, times((first[0][rows], first[1][rows]), split(turn))


def entering(run, u, t):
    lefts, rights = [u], [t]
    for k in range(run.count - 1):
        b = run.block(1, 0, k)
        lefts.append(b if lefts[-1] is None else b + times(run.wide_block(0, k), split(lefts[-1])))
    for k in range(run.count - 1, 0, -1):
        term = run.block(1, 1, k) + times(run.wide_block(1, k), split(lefts[k]))
        rights.append(term if rights[-1] is None else term + times(run.wide_c(k), split(rights[-1])))
    return lefts, rights[::-1]


def chosen(options, index):
    result = options[0]
    for k, option in enumerate(options[1:], 1):
        result = jnp.where(index == k, option, result)
    return result


def gathered_run(own, other, half, rows):
    halves = (own, other) if half == 0 else (other, own)
    return Run(lambda h, k: halves[h].at[k], own.shape[0], rows)


def leaf_run(own, other, half, rows):
    sides = (own, other) if half == 0 else (other, own)
    return Run(lambda h, k: sides[k].at[h], 2, rows)


def leaf_kernel(factor, link, vectors, out, tops, bottoms, link_here, vectors_here, sems):
    rows, orbitals = link.shape[0], factor.shape[1]
    last = orbitals - rows
    copies = [
        pltpu.make_async_copy(link, link_here, sems.at[0]),
        pltpu.make_async_copy(vectors, vectors_here, sems.at[1]),
    ]
    for part in (0, 1):
        copies.append(
            pltpu.make_async_copy(factor.at[part, pl.ds(0, rows)], tops.at[part], sems.at[2 + part])
        )
        copies.append(
            pltpu.make_async_copy(factor.at[part, pl.ds(last, rows)], bottoms.at[part], sems.at[4 + part])
        )
    for copy in copies:
        copy.start()
    for copy in copies:
        copy.wait()
    v, v_t = split(link_here[...]), split(link_here[...].T)
    y = vectors_here[...]
    for part in (0, 1):
        low, high = tops[part], bottoms[part]
        at = slice(part * rows, (part + 1) * rows)
        left = high[:, :rows]
        out[0, at, :] = dot(v_t[0], left) + dot(v_t[1], left)
        out[1, at, :] = times(v_t, split(dot(high, y)))
        at = slice((2 + part) * rows, (3 + part) * rows)
        out[0, at, :] = low[:, :rows].astype(F32)
        out[1, at, :] = dot(low, y)
        right = low[:, last:]
        out[part, 4 * rows :, :] = dot(right, v[0]) + dot(right, v[1])


def merge_kernel(make, place, own, other, out):
    rows = out.shape[1] // 5
    for half in (0, 1):

        @pl.when(place[0] == half)
        def _():
            new_x, new_w, new_c = merged(make(own, other, half, rows), half)
            for k in range(out.shape[0]):
                out[k, : 2 * rows, :] = new_x
                out[k, 2 * rows : 4 * rows, :] = new_w
                out[k, 4 * rows :, :] = new_c


def down_kernel(place, weight, factor, link, vectors, leaf, leaf_2, rank, rank_2, file, file_2, out):
    rows, columns = link.shape
    orbitals = factor.shape[1]
    zero = jnp.zeros((2 * rows, columns), F32)

    def sweep(half):
        lefts, rights = entering(gathered_run(file, file_2, half, rows), None, None)
        u, t = chosen([zero] + lefts[1:], place[2]), chosen(rights[:-1] + [zero], place[2])
        lefts, rights = entering(gathered_run(rank, rank_2, half, rows), u, t)
        u, t = chosen(lefts, place[1]), chosen(rights, place[1])
        lefts, rights = entering(leaf_run(leaf, leaf_2, half, rows), u, t)
        u, t = lefts[half], rights[half]
        w_re, w_im = weight[0, 0], weight[0, 1]
        turned = (w_re * u[:rows] - w_im * u[rows:], w_re * u[rows:] + w_im * u[:rows])
        after = (w_re * t[:rows] - w_im * t[rows:], w_re * t[rows:] + w_im * t[:rows])
        v = split(link[...])
        y = vectors[...].astype(F32)
        total = None
        for part, w in ((0, w_re), (1, -w_im)):
            sign = 1.0 if part == 0 else -1.0
            field = w * y
            moved = times(v, split(after[part]))
            field = jnp.concatenate(
                [
                    field[:rows] + sign * turned[part],
                    field[rows : orbitals - rows],
                    field[orbitals - rows :] + sign * moved,
                ],
                0,
            )
            high, low = split(field)
            f = factor[part]
            term = dot(f, high) + dot(f, low)
            total = term if total is None else total + term
        count = out.shape[0]
        share, spare = orbitals // count, rows // count
        for q in range(count):
            out[q, :share, :] = total[q * share : (q + 1) * share]
            out[q, share:, :] = after[0][q * spare : (q + 1) * spare]

    for half in (0, 1):

        @pl.when(place[0] == half)
        def _():
            sweep(half)


def sum_kernel(terms, spread, share_out):
    total = jnp.sum(terms[...], 0)
    for q in range(spread.shape[0]):
        spread[q] = total
    share_out[...] = total[: share_out.shape[0]]


def pair_kernel(place, both, spread):
    total = both[0, place[0]] + both[1, place[0]]
    for k in range(spread.shape[0]):
        spread[k] = total


def tile_kernel(field, onsite, link, out):
    columns = field.shape[2]
    orbitals, rows = onsite.shape[0], link.shape[0]
    share = orbitals // field.shape[0]
    whole = field[:, :share, :].reshape(orbitals, columns)
    following = field[:, share:, :].reshape(rows, columns)
    parts = split(whole)
    weighted = 0.5 * times(split(onsite[...]), parts)
    coupled = times(split(link[...]), split(following))
    weighted = jnp.concatenate([weighted[: orbitals - rows], weighted[orbitals - rows :] + coupled], 0)
    flipped = tuple(p.T for p in parts)
    gram = times(flipped, parts)
    tile = times(flipped, split(weighted))
    tile = tile + tile.T
    row = lax.broadcasted_iota(jnp.int32, gram.shape, 0)
    col = lax.broadcasted_iota(jnp.int32, gram.shape, 1)
    packed = jnp.where(row <= col, gram, tile)
    middle = jnp.sum(jnp.where(row == col, tile, 0.0), 0, keepdims=True)
    half = columns // 2
    for h in (0, 1):
        out[h, :half, :] = packed[h * half : (h + 1) * half]
        out[h, half:, :] = jnp.broadcast_to(middle, (8, columns))


def final_kernel(scale, halves, gram_out, tile_out):
    columns = gram_out.shape[1]
    half = columns // 2
    packed = jnp.concatenate([halves[0, :half, :], halves[1, :half, :]], 0) * scale
    middle = jnp.broadcast_to(halves[0, half : half + 1, :] * scale, packed.shape)
    flipped = packed.T
    row = lax.broadcasted_iota(jnp.int32, packed.shape, 0)
    col = lax.broadcasted_iota(jnp.int32, packed.shape, 1)
    gram_out[...] = jnp.where(row <= col, packed, flipped)
    tile_out[...] = jnp.where(row == col, middle, jnp.where(row > col, packed, flipped))


SMEM = pl.BlockSpec(memory_space=pltpu.SMEM)
VMEM = pl.BlockSpec(memory_space=pltpu.VMEM)
ANY = pl.BlockSpec(memory_space=pltpu.HBM)


def call(kernel, shapes, specs, *args, scratch=(), room=VMEM_BYTES):
    shapes = [jax.ShapeDtypeStruct(s, F32) for s in shapes]
    single = len(shapes) == 1
    return pl.pallas_call(
        kernel,
        out_shape=shapes[0] if single else shapes,
        in_specs=specs,
        out_specs=VMEM if single else [VMEM] * len(shapes),
        scratch_shapes=list(scratch),
        compiler_params=pltpu.CompilerParams(vmem_limit_bytes=room),
        cost_estimate=pl.CostEstimate(flops=1 << 26, bytes_accessed=1 << 20, transcendentals=0),
    )(*args)


def swapped(x):
    return lax.ppermute(x, "core", [(0, 1), (1, 0)])


def exchanged(x, axes):
    return lax.all_to_all(x, axes, 0, 0, tiled=True)


def per_device(factors, onsite, coupling, vectors, quad_weight):
    factor, link, here = factors[0, 0], coupling[0], vectors[0]
    orbitals, columns = here.shape
    rows = link.shape[0]
    quads = lax.axis_size("quad")
    place = jnp.stack([lax.axis_index(a) for a in ("core", "x", "y")]).astype(jnp.int32)
    half_map = (5 * rows, columns)

    leaf = call(
        leaf_kernel,
        [(2, *half_map)],
        [ANY] * 3,
        factor,
        link,
        here,
        scratch=[
            pltpu.VMEM((2, rows, orbitals), BF16),
            pltpu.VMEM((2, rows, orbitals), BF16),
            pltpu.VMEM(link.shape, F32),
            pltpu.VMEM(here.shape, BF16),
            pltpu.SemaphoreType.DMA((6,)),
        ],
    )
    levels = [leaf, swapped(leaf)]
    for axis, make in (("x", leaf_run), ("y", gathered_run)):
        mine = call(
            functools.partial(merge_kernel, make),
            [(lax.axis_size(axis), *half_map)],
            [SMEM, VMEM, VMEM],
            place,
            *levels[-2:],
        )
        own = exchanged(mine, axis)
        levels += [own, swapped(own)]

    share = orbitals // quads
    rows_sent = share + rows // quads
    terms = call(
        down_kernel,
        [(quads, rows_sent, columns)],
        [SMEM, SMEM] + [VMEM] * (3 + len(levels)),
        place,
        quad_weight,
        factor,
        link,
        here,
        *levels,
    )
    spread, subspace = call(
        sum_kernel,
        [(quads, rows_sent, columns), (share, columns)],
        [VMEM],
        exchanged(terms, "quad"),
    )
    field = exchanged(spread, "quad")
    packed = (columns // 2 + 8, columns)
    tiles = call(tile_kernel, [(2, *packed)], [VMEM] * 3, field, onsite[0], link)
    plane = SLAB[:2]
    spread = call(
        pair_kernel,
        [(lax.axis_size(plane), *packed)],
        [SMEM, VMEM],
        place,
        lax.all_gather(tiles, "core"),
    )
    halves = lax.all_gather(jnp.sum(exchanged(spread, plane), axis=0), "core")
    scale = 1.0 / (orbitals * lax.axis_size(SLAB))
    correlation, projected = call(
        functools.partial(final_kernel, scale), [(columns, columns)] * 2, [VMEM], halves
    )
    return subspace[None], correlation, projected


def solution(mesh):
    torus = Mesh(mesh.devices.reshape(mesh.shape["quad"], 4, 4, 2), ("quad", *SLAB))
    return jax.shard_map(
        per_device,
        mesh=torus,
        in_specs=(
            P("quad", SLAB, None, None, None),
            P(SLAB, None, None),
            P(SLAB, None, None),
            P(SLAB, None, None),
            P("quad", None),
        ),
        out_specs=(P(SLAB, "quad", None), P(), P()),
        check_vma=False,
    )
```

```python
import functools

import jax
import jax.numpy as jnp
from jax import lax
from jax.experimental import pallas as pl
from jax.experimental.pallas import tpu as pltpu
from jax.sharding import Mesh
from jax.sharding import PartitionSpec as P

F32 = jnp.float32
BF16 = jnp.bfloat16
SLAB = ("y", "x", "core")
VMEM_BYTES = 24 << 20


def split(x):
    high = x.astype(BF16)
    return high, (x - high.astype(F32)).astype(BF16)


def dot(a, b):
    return jnp.dot(a, b, preferred_element_type=F32)


def times(left, right):
    return dot(left[0], right[0]) + (dot(left[0], right[1]) + dot(left[1], right[0]))


def wide(real, imag):
    return tuple(
        jnp.concatenate([jnp.concatenate([r, i], 1), jnp.concatenate([-i, r], 1)], 0)
        for r, i in zip(split(real), split(imag))
    )


class Run:
    def __init__(self, get, count, rows):
        self.get, self.count, self.rows = get, count, rows

    def part(self, half, block, k):
        return self.get(half, k)[block * self.rows : (block + 1) * self.rows, :]

    def state(self, half, which, k):
        return jnp.concatenate([self.part(half, 2 * which + p, k) for p in (0, 1)], 1)

    def wide(self, which, k):
        return wide(self.part(0, 2 * which, k), self.part(0, 2 * which + 1, k))

    def wide_c(self, k):
        return wide(self.part(0, 4, k), self.part(1, 4, k))


def merged(run, half):
    rows, last = run.rows, run.count - 1
    states = [run.state(half, 0, 0)]
    for k in range(1, run.count):
        state = times(split(states[-1]), run.wide(0, k))
        states.append(state + run.state(1, 0, k) if half else state)

    def from_left(k):
        term = times(split(states[k - 1]), run.wide(1, k))
        return term + run.state(1, 1, k) if half else term

    back = from_left(last)
    turn = jnp.concatenate([run.part(0, 4, last), run.part(1, 4, last)], 1)
    columns = back.shape[0]
    for k in range(last - 1, 0, -1):
        both = times(split(jnp.concatenate([back, turn], 0)), run.wide_c(k))
        back, turn = both[:columns] + from_left(k), both[columns:]
    first = run.wide_c(0)
    back = run.state(half, 1, 0) + times(split(back), first)
    at = slice(half * rows, (half + 1) * rows)
    turn = times(split(turn), (first[0][:, at], first[1][:, at]))
    ahead = states[-1]
    return ahead[:, :rows], ahead[:, rows:], back[:, :rows], back[:, rows:], turn


def entering(run, u, t):
    lefts, rights = [u], [t]
    for k in range(run.count - 1):
        b = run.state(1, 0, k)
        lefts.append(b if lefts[-1] is None else b + times(split(lefts[-1]), run.wide(0, k)))
    for k in range(run.count - 1, 0, -1):
        term = run.state(1, 1, k) + times(split(lefts[k]), run.wide(1, k))
        rights.append(term if rights[-1] is None else term + times(split(rights[-1]), run.wide_c(k)))
    return lefts, rights[::-1]


def chosen(options, index):
    result = options[0]
    for k, option in enumerate(options[1:], 1):
        result = jnp.where(index == k, option, result)
    return result


def gathered_run(own, other, half, rows):
    halves = (own, other) if half == 0 else (other, own)
    return Run(lambda h, k: halves[h].at[k], own.shape[0], rows)


def leaf_run(own, other, half, rows):
    sides = (own, other) if half == 0 else (other, own)
    return Run(lambda h, k: sides[k].at[h], 2, rows)


def leaf_kernel(factor, link, vectors, out, tops, bottoms, link_here, vectors_here, sems):
    rows, orbitals = link.shape[0], factor.shape[1]
    last = orbitals - rows
    copies = [
        pltpu.make_async_copy(link, link_here, sems.at[0]),
        pltpu.make_async_copy(vectors, vectors_here, sems.at[1]),
    ]
    for part in (0, 1):
        copies.append(
            pltpu.make_async_copy(factor.at[part, pl.ds(0, rows)], tops.at[part], sems.at[2 + part])
        )
        copies.append(
            pltpu.make_async_copy(factor.at[part, pl.ds(last, rows)], bottoms.at[part], sems.at[4 + part])
        )
    for copy in copies:
        copy.start()
    copies[0].wait()
    v, v_t = split(link_here[...]), split(link_here[...].T)
    copies[1].wait()
    y = vectors_here[...]
    for part in (0, 1):
        copies[2 + 2 * part].wait()
        copies[3 + 2 * part].wait()
        low, high = tops[part], bottoms[part]
        at = slice(part * rows, (part + 1) * rows)
        left = high[:, :rows]
        out[0, at, :] = (dot(v_t[0], left) + dot(v_t[1], left)).T
        out[1, at, :] = times(v_t, split(dot(high, y))).T
        at = slice((2 + part) * rows, (3 + part) * rows)
        out[0, at, :] = low[:, :rows].astype(F32).T
        out[1, at, :] = dot(low, y).T
        right = low[:, last:]
        out[part, 4 * rows :, :] = (dot(right, v[0]) + dot(right, v[1])).T


def merge_kernel(make, place, own, other, out):
    rows = out.shape[1] // 5
    for half in (0, 1):

        @pl.when(place[0] == half)
        def _():
            blocks = merged(make(own, other, half, rows), half)
            for k in range(out.shape[0]):
                for n, block in enumerate(blocks):
                    out[k, n * rows : (n + 1) * rows, :] = block


def down_kernel(place, weight, factor, link, vectors, leaf, leaf_2, rank, rank_2, file, file_2, out):
    rows, columns = link.shape
    orbitals = factor.shape[1]
    zero = jnp.zeros((columns, 2 * rows), F32)

    def sweep(half):
        lefts, rights = entering(gathered_run(file, file_2, half, rows), None, None)
        u, t = chosen([zero] + lefts[1:], place[2]), chosen(rights[:-1] + [zero], place[2])
        lefts, rights = entering(gathered_run(rank, rank_2, half, rows), u, t)
        u, t = chosen(lefts, place[1]), chosen(rights, place[1])
        lefts, rights = entering(leaf_run(leaf, leaf_2, half, rows), u, t)
        u, t = lefts[half], rights[half]
        w_re, w_im = weight[0, 0], weight[0, 1]
        turned, after = (
            ((w_re * x[:, :rows] - w_im * x[:, rows:]).T, (w_re * x[:, rows:] + w_im * x[:, :rows]).T)
            for x in (u, t)
        )
        v = split(link[...])
        y = vectors[...].astype(F32)
        total = None
        for part, w in ((0, w_re), (1, -w_im)):
            sign = 1.0 if part == 0 else -1.0
            field = w * y
            moved = times(v, split(after[part]))
            field = jnp.concatenate(
                [
                    field[:rows] + sign * turned[part],
                    field[rows : orbitals - rows],
                    field[orbitals - rows :] + sign * moved,
                ],
                0,
            )
            high, low = split(field)
            f = factor[part]
            term = dot(f, high) + dot(f, low)
            total = term if total is None else total + term
        count = out.shape[0]
        share, spare = orbitals // count, rows // count
        for q in range(count):
            out[q, :share, :] = total[q * share : (q + 1) * share]
            out[q, share:, :] = after[0][q * spare : (q + 1) * spare]

    for half in (0, 1):

        @pl.when(place[0] == half)
        def _():
            sweep(half)


def sum_kernel(terms, spread, share_out):
    total = jnp.sum(terms[...], 0)
    for q in range(spread.shape[0]):
        spread[q] = total
    share_out[...] = total[: share_out.shape[0]]


def pair_kernel(place, both, spread):
    total = both[0, place[0]] + both[1, place[0]]
    for k in range(spread.shape[0]):
        spread[k] = total


def tile_kernel(field, onsite, link, out):
    columns = field.shape[2]
    orbitals, rows = onsite.shape[0], link.shape[0]
    share = orbitals // field.shape[0]
    whole = field[:, :share, :].reshape(orbitals, columns)
    following = field[:, share:, :].reshape(rows, columns)
    parts = split(whole)
    weighted = 0.5 * times(split(onsite[...]), parts)
    coupled = times(split(link[...]), split(following))
    weighted = jnp.concatenate([weighted[: orbitals - rows], weighted[orbitals - rows :] + coupled], 0)
    flipped = tuple(p.T for p in parts)
    gram = times(flipped, parts)
    tile = times(flipped, split(weighted))
    tile = tile + tile.T
    row = lax.broadcasted_iota(jnp.int32, gram.shape, 0)
    col = lax.broadcasted_iota(jnp.int32, gram.shape, 1)
    packed = jnp.where(row <= col, gram, tile)
    middle = jnp.sum(jnp.where(row == col, tile, 0.0), 0, keepdims=True)
    half = columns // 2
    for h in (0, 1):
        out[h, :half, :] = packed[h * half : (h + 1) * half]
        out[h, half:, :] = jnp.broadcast_to(middle, (8, columns))


def final_kernel(scale, halves, gram_out, tile_out):
    columns = gram_out.shape[1]
    half = columns // 2
    packed = jnp.concatenate([halves[0, :half, :], halves[1, :half, :]], 0) * scale
    middle = jnp.broadcast_to(halves[0, half : half + 1, :] * scale, packed.shape)
    flipped = packed.T
    row = lax.broadcasted_iota(jnp.int32, packed.shape, 0)
    col = lax.broadcasted_iota(jnp.int32, packed.shape, 1)
    gram_out[...] = jnp.where(row <= col, packed, flipped)
    tile_out[...] = jnp.where(row == col, middle, jnp.where(row > col, packed, flipped))


SMEM = pl.BlockSpec(memory_space=pltpu.SMEM)
VMEM = pl.BlockSpec(memory_space=pltpu.VMEM)
HBM = pl.BlockSpec(memory_space=pltpu.HBM)


def call(kernel, shapes, specs, *args, scratch=(), room=VMEM_BYTES):
    shapes = [jax.ShapeDtypeStruct(s, F32) for s in shapes]
    single = len(shapes) == 1
    return pl.pallas_call(
        kernel,
        out_shape=shapes[0] if single else shapes,
        in_specs=specs,
        out_specs=VMEM if single else [VMEM] * len(shapes),
        scratch_shapes=list(scratch),
        compiler_params=pltpu.CompilerParams(vmem_limit_bytes=room),
        cost_estimate=pl.CostEstimate(flops=1 << 26, bytes_accessed=1 << 20, transcendentals=0),
    )(*args)


def swapped(x):
    return lax.ppermute(x, "core", [(0, 1), (1, 0)])


def exchanged(x, axes):
    return lax.all_to_all(x, axes, 0, 0, tiled=True)


def per_device(factors, onsite, coupling, vectors, quad_weight):
    factor, link, here = factors[0, 0], coupling[0], vectors[0]
    orbitals, columns = here.shape
    rows = link.shape[0]
    quads = lax.axis_size("quad")
    place = jnp.stack([lax.axis_index(a) for a in ("core", "x", "y")]).astype(jnp.int32)
    half_map = (5 * rows, columns)

    leaf = call(
        leaf_kernel,
        [(2, *half_map)],
        [HBM] * 3,
        *(pltpu.with_memory_space_constraint(a, pltpu.HBM) for a in (factor, link, here)),
        scratch=[
            pltpu.VMEM((2, rows, orbitals), BF16),
            pltpu.VMEM((2, rows, orbitals), BF16),
            pltpu.VMEM(link.shape, F32),
            pltpu.VMEM(here.shape, BF16),
            pltpu.SemaphoreType.DMA((6,)),
        ],
    )
    levels = [leaf, swapped(leaf)]
    for axis, make in (("x", leaf_run), ("y", gathered_run)):
        mine = call(
            functools.partial(merge_kernel, make),
            [(lax.axis_size(axis), *half_map)],
            [SMEM, VMEM, VMEM],
            place,
            *levels[-2:],
        )
        own = exchanged(mine, axis)
        levels += [own, swapped(own)]

    share = orbitals // quads
    rows_sent = share + rows // quads
    terms = call(
        down_kernel,
        [(quads, rows_sent, columns)],
        [SMEM, SMEM] + [VMEM] * (3 + len(levels)),
        place,
        quad_weight,
        factor,
        link,
        here,
        *levels,
    )
    spread, subspace = call(
        sum_kernel,
        [(quads, rows_sent, columns), (share, columns)],
        [VMEM],
        exchanged(terms, "quad"),
    )
    field = exchanged(spread, "quad")
    packed = (columns // 2 + 8, columns)
    tiles = call(tile_kernel, [(2, *packed)], [VMEM] * 3, field, onsite[0], link)
    plane = SLAB[:2]
    spread = call(
        pair_kernel,
        [(lax.axis_size(plane), *packed)],
        [SMEM, VMEM],
        place,
        lax.all_gather(tiles, "core"),
    )
    halves = lax.all_gather(jnp.sum(exchanged(spread, plane), axis=0), "core")
    scale = 1.0 / (orbitals * lax.axis_size(SLAB))
    correlation, projected = call(
        functools.partial(final_kernel, scale), [(columns, columns)] * 2, [VMEM], halves
    )
    return subspace[None], correlation, projected


def solution(mesh):
    torus = Mesh(mesh.devices.reshape(mesh.shape["quad"], 4, 4, 2), ("quad", *SLAB))
    return jax.shard_map(
        per_device,
        mesh=torus,
        in_specs=(
            P("quad", SLAB, None, None, None),
            P(SLAB, None, None),
            P(SLAB, None, None),
            P(SLAB, None, None),
            P("quad", None),
        ),
        out_specs=(P(SLAB, "quad", None), P(), P()),
        check_vma=False,
    )
```

```python
import functools

import jax
import jax.numpy as jnp
from jax import lax
from jax.experimental import pallas as pl
from jax.experimental.pallas import tpu as pltpu
from jax.sharding import Mesh
from jax.sharding import PartitionSpec as P

F32 = jnp.float32
BF16 = jnp.bfloat16
SLAB = ("y", "x", "core")
VMEM_BYTES = 24 << 20


def split(x):
    high = x.astype(BF16)
    return high, (x - high.astype(F32)).astype(BF16)


def dot(a, b):
    return jnp.dot(a, b, preferred_element_type=F32)


def times(left, right):
    return dot(left[0], right[0]) + (dot(left[0], right[1]) + dot(left[1], right[0]))


def wide(real, imag):
    return tuple(
        jnp.concatenate([jnp.concatenate([r, i], 1), jnp.concatenate([-i, r], 1)], 0)
        for r, i in zip(split(real), split(imag))
    )


class Run:
    def __init__(self, get, count, rows):
        self.get, self.count, self.rows = get, count, rows

    def part(self, half, block, k):
        return self.get(half, k)[block * self.rows : (block + 1) * self.rows, :]

    def state(self, half, which, k):
        return jnp.concatenate([self.part(half, 2 * which + p, k) for p in (0, 1)], 1)

    def wide(self, which, k):
        return wide(self.part(0, 2 * which, k), self.part(0, 2 * which + 1, k))

    def wide_c(self, k):
        return wide(self.part(0, 4, k), self.part(1, 4, k))


def merged(run, half):
    rows, last = run.rows, run.count - 1
    states = [run.state(half, 0, 0)]
    for k in range(1, run.count):
        state = times(split(states[-1]), run.wide(0, k))
        states.append(state + run.state(1, 0, k) if half else state)

    def from_left(k):
        term = times(split(states[k - 1]), run.wide(1, k))
        return term + run.state(1, 1, k) if half else term

    back = from_left(last)
    turn = jnp.concatenate([run.part(0, 4, last), run.part(1, 4, last)], 1)
    columns = back.shape[0]
    for k in range(last - 1, 0, -1):
        both = times(split(jnp.concatenate([back, turn], 0)), run.wide_c(k))
        back, turn = both[:columns] + from_left(k), both[columns:]
    first = run.wide_c(0)
    back = run.state(half, 1, 0) + times(split(back), first)
    at = slice(half * rows, (half + 1) * rows)
    turn = times(split(turn), (first[0][:, at], first[1][:, at]))
    ahead = states[-1]
    return ahead[:, :rows], ahead[:, rows:], back[:, :rows], back[:, rows:], turn


def entering(run, u, t):
    lefts, rights = [u], [t]
    for k in range(run.count - 1):
        b = run.state(1, 0, k)
        lefts.append(b if lefts[-1] is None else b + times(split(lefts[-1]), run.wide(0, k)))
    for k in range(run.count - 1, 0, -1):
        term = run.state(1, 1, k) + times(split(lefts[k]), run.wide(1, k))
        rights.append(term if rights[-1] is None else term + times(split(rights[-1]), run.wide_c(k)))
    return lefts, rights[::-1]


def chosen(options, index):
    result = options[0]
    for k, option in enumerate(options[1:], 1):
        result = jnp.where(index == k, option, result)
    return result


def gathered_run(own, other, half, rows):
    halves = (own, other) if half == 0 else (other, own)
    return Run(lambda h, k: halves[h].at[k], own.shape[0], rows)


def leaf_run(own, other, half, rows):
    sides = (own, other) if half == 0 else (other, own)
    return Run(lambda h, k: sides[k].at[h], 2, rows)


def leaf_kernel(factor, link, vectors, out, tops, bottoms, link_here, vectors_here, sems):
    rows, orbitals = link.shape[0], factor.shape[1]
    last = orbitals - rows
    copies = [
        pltpu.make_async_copy(link, link_here, sems.at[0]),
        pltpu.make_async_copy(vectors, vectors_here, sems.at[1]),
    ]
    for part in (0, 1):
        copies.append(
            pltpu.make_async_copy(factor.at[part, pl.ds(0, rows)], tops.at[part], sems.at[2 + part])
        )
        copies.append(
            pltpu.make_async_copy(factor.at[part, pl.ds(last, rows)], bottoms.at[part], sems.at[4 + part])
        )
    for copy in copies:
        copy.start()
    copies[0].wait()
    v, v_t = split(link_here[...]), split(link_here[...].T)
    copies[1].wait()
    y = vectors_here[...]
    for part in (0, 1):
        copies[2 + 2 * part].wait()
        copies[3 + 2 * part].wait()
        low, high = tops[part], bottoms[part]
        at = slice(part * rows, (part + 1) * rows)
        left = high[:, :rows]
        out[0, at, :] = (dot(v_t[0], left) + dot(v_t[1], left)).T
        out[1, at, :] = times(v_t, split(dot(high, y))).T
        at = slice((2 + part) * rows, (3 + part) * rows)
        out[0, at, :] = low[:, :rows].astype(F32).T
        out[1, at, :] = dot(low, y).T
        right = low[:, last:]
        out[part, 4 * rows :, :] = (dot(right, v[0]) + dot(right, v[1])).T


def merge_kernel(make, place, own, other, out):
    rows = out.shape[1] // 5
    for half in (0, 1):

        @pl.when(place[0] == half)
        def _():
            blocks = merged(make(own, other, half, rows), half)
            for k in range(out.shape[0]):
                for n, block in enumerate(blocks):
                    out[k, n * rows : (n + 1) * rows, :] = block


def base_kernel(weight, factor, vectors, out):
    y = vectors[...].astype(F32)
    real, imag = split(weight[0, 0] * y), split(-weight[0, 1] * y)
    out[...] = (dot(factor[0], real[0]) + dot(factor[0], real[1])) + (
        dot(factor[1], imag[0]) + dot(factor[1], imag[1])
    )


def inner_kernel(place, leaf, leaf_2, rank, rank_2, out):
    rows = out.shape[0] // 10
    one = jnp.where(
        lax.broadcasted_iota(jnp.int32, (rows, rows), 0) == lax.broadcasted_iota(jnp.int32, (rows, rows), 1),
        1.0,
        0.0,
    )
    none = jnp.zeros((rows, rows), F32)
    unit, zero = jnp.concatenate([one, none], 1), jnp.zeros((rows, 2 * rows), F32)

    def stacked(*parts):
        return jnp.concatenate(parts, 0)

    def build(half):
        run = gathered_run(rank, rank_2, half, rows)
        last = run.count - 1
        lefts = [stacked(unit, zero), stacked(run.state(0, 0, 0), run.state(1, 0, 0))]
        for k in range(1, last):
            state = times(split(lefts[-1]), run.wide(0, k))
            lefts.append(state + stacked(zero, run.state(1, 0, k)))
        rights = [stacked(zero, zero, unit)]
        for k in range(last, 0, -1):
            term = times(split(lefts[k]), run.wide(1, k)) + stacked(zero, run.state(1, 1, k))
            turn = jnp.concatenate([run.part(0, 4, k), run.part(1, 4, k)], 1)
            if k == last:
                rights.append(stacked(term, turn))
            else:
                rights.append(times(split(rights[-1]), run.wide_c(k)) + stacked(term, zero))
        u, t = chosen(lefts, place[1]), chosen(rights[::-1], place[1])
        pair = leaf_run(leaf, leaf_2, half, rows)
        mid = times(split(u), pair.wide(0, 0)) + stacked(zero, pair.state(1, 0, 0))
        if half:
            u = mid
        else:
            term = times(split(mid), pair.wide(1, 1)) + stacked(zero, pair.state(1, 1, 1))
            t = times(split(t), pair.wide_c(1)) + stacked(term, zero)
        whole = stacked(u, t)
        for n in range(5):
            for p in (0, 1):
                at = (2 * n + p) * rows
                out[at : at + rows, :] = whole[n * rows : (n + 1) * rows, p * rows : (p + 1) * rows]

    for half in (0, 1):

        @pl.when(place[0] == half)
        def _():
            build(half)


def down_kernel(place, weight, factor, link, base, inner, file, file_2, out):
    rows, columns = link.shape
    orbitals = factor.shape[1]
    zero = jnp.zeros((columns, 2 * rows), F32)

    def block(n):
        return inner[2 * n * rows : (2 * n + 1) * rows, :], inner[(2 * n + 1) * rows : (2 * n + 2) * rows, :]

    def sweep(half):
        lefts, rights = entering(gathered_run(file, file_2, half, rows), None, None)
        u = split(chosen([zero] + lefts[1:], place[2]))
        t = split(chosen(rights[:-1] + [zero], place[2]))
        t = jnp.concatenate(block(3), 1) + (times(t, wide(*block(4))) + times(u, wide(*block(2))))
        u = jnp.concatenate(block(1), 1) + times(u, wide(*block(0)))
        w_re, w_im = weight[0, 0], weight[0, 1]
        turned, after = (
            ((w_re * x[:, :rows] - w_im * x[:, rows:]).T, (w_re * x[:, rows:] + w_im * x[:, :rows]).T)
            for x in (u, t)
        )
        v = split(link[...])
        total = base[...]
        for part, sign in ((0, 1.0), (1, -1.0)):
            f = factor[part]
            for field, cols in (
                (turned[part], slice(0, rows)),
                (times(v, split(after[part])), slice(orbitals - rows, orbitals)),
            ):
                high, low = split(sign * field)
                total = total + (dot(f[:, cols], high) + dot(f[:, cols], low))
        count = out.shape[0]
        share, spare = orbitals // count, rows // count
        for q in range(count):
            out[q, :share, :] = total[q * share : (q + 1) * share]
            out[q, share:, :] = after[0][q * spare : (q + 1) * spare]

    for half in (0, 1):

        @pl.when(place[0] == half)
        def _():
            sweep(half)


def sum_kernel(terms, spread, share_out):
    total = jnp.sum(terms[...], 0)
    for q in range(spread.shape[0]):
        spread[q] = total
    share_out[...] = total[: share_out.shape[0]]


def pair_kernel(place, both, spread):
    total = both[0, place[0]] + both[1, place[0]]
    for k in range(spread.shape[0]):
        spread[k] = total


def tile_kernel(field, onsite, link, out):
    columns = field.shape[2]
    orbitals, rows = onsite.shape[0], link.shape[0]
    share = orbitals // field.shape[0]
    whole = field[:, :share, :].reshape(orbitals, columns)
    following = field[:, share:, :].reshape(rows, columns)
    parts = split(whole)
    weighted = 0.5 * times(split(onsite[...]), parts)
    coupled = times(split(link[...]), split(following))
    weighted = jnp.concatenate([weighted[: orbitals - rows], weighted[orbitals - rows :] + coupled], 0)
    flipped = tuple(p.T for p in parts)
    gram = times(flipped, parts)
    tile = times(flipped, split(weighted))
    tile = tile + tile.T
    row = lax.broadcasted_iota(jnp.int32, gram.shape, 0)
    col = lax.broadcasted_iota(jnp.int32, gram.shape, 1)
    packed = jnp.where(row <= col, gram, tile)
    middle = jnp.sum(jnp.where(row == col, tile, 0.0), 0, keepdims=True)
    half = columns // 2
    for h in (0, 1):
        out[h, :half, :] = packed[h * half : (h + 1) * half]
        out[h, half:, :] = jnp.broadcast_to(middle, (8, columns))


def final_kernel(scale, halves, gram_out, tile_out):
    columns = gram_out.shape[1]
    half = columns // 2
    packed = jnp.concatenate([halves[0, :half, :], halves[1, :half, :]], 0) * scale
    middle = jnp.broadcast_to(halves[0, half : half + 1, :] * scale, packed.shape)
    flipped = packed.T
    row = lax.broadcasted_iota(jnp.int32, packed.shape, 0)
    col = lax.broadcasted_iota(jnp.int32, packed.shape, 1)
    gram_out[...] = jnp.where(row <= col, packed, flipped)
    tile_out[...] = jnp.where(row == col, middle, jnp.where(row > col, packed, flipped))


SMEM = pl.BlockSpec(memory_space=pltpu.SMEM)
VMEM = pl.BlockSpec(memory_space=pltpu.VMEM)
HBM = pl.BlockSpec(memory_space=pltpu.HBM)


def call(kernel, shapes, specs, *args, scratch=(), room=VMEM_BYTES):
    shapes = [jax.ShapeDtypeStruct(s, F32) for s in shapes]
    single = len(shapes) == 1
    return pl.pallas_call(
        kernel,
        out_shape=shapes[0] if single else shapes,
        in_specs=specs,
        out_specs=VMEM if single else [VMEM] * len(shapes),
        scratch_shapes=list(scratch),
        compiler_params=pltpu.CompilerParams(vmem_limit_bytes=room),
        cost_estimate=pl.CostEstimate(flops=1 << 26, bytes_accessed=1 << 20, transcendentals=0),
    )(*args)


def swapped(x):
    return lax.ppermute(x, "core", [(0, 1), (1, 0)])


def exchanged(x, axes):
    return lax.all_to_all(x, axes, 0, 0, tiled=True)


def per_device(factors, onsite, coupling, vectors, quad_weight):
    factor, link, here = factors[0, 0], coupling[0], vectors[0]
    orbitals, columns = here.shape
    rows = link.shape[0]
    quads = lax.axis_size("quad")
    place = jnp.stack([lax.axis_index(a) for a in ("core", "x", "y")]).astype(jnp.int32)
    half_map = (5 * rows, columns)

    leaf = call(
        leaf_kernel,
        [(2, *half_map)],
        [HBM] * 3,
        *(pltpu.with_memory_space_constraint(a, pltpu.HBM) for a in (factor, link, here)),
        scratch=[
            pltpu.VMEM((2, rows, orbitals), BF16),
            pltpu.VMEM((2, rows, orbitals), BF16),
            pltpu.VMEM(link.shape, F32),
            pltpu.VMEM(here.shape, BF16),
            pltpu.SemaphoreType.DMA((6,)),
        ],
    )
    levels = [leaf, swapped(leaf)]
    for axis, make in (("x", leaf_run), ("y", gathered_run)):
        mine = call(
            functools.partial(merge_kernel, make),
            [(lax.axis_size(axis), *half_map)],
            [SMEM, VMEM, VMEM],
            place,
            *levels[-2:],
        )
        own = exchanged(mine, axis)
        levels += [own, swapped(own)]

    share = orbitals // quads
    rows_sent = share + rows // quads
    base = call(base_kernel, [(orbitals, columns)], [SMEM, VMEM, VMEM], quad_weight, factor, here)
    inner = call(inner_kernel, [(10 * rows, rows)], [SMEM] + [VMEM] * 4, place, *levels[:4])
    terms = call(
        down_kernel,
        [(quads, rows_sent, columns)],
        [SMEM, SMEM] + [VMEM] * 6,
        place,
        quad_weight,
        factor,
        link,
        base,
        inner,
        *levels[4:],
    )
    spread, subspace = call(
        sum_kernel,
        [(quads, rows_sent, columns), (share, columns)],
        [VMEM],
        exchanged(terms, "quad"),
    )
    field = exchanged(spread, "quad")
    packed = (columns // 2 + 8, columns)
    tiles = call(tile_kernel, [(2, *packed)], [VMEM] * 3, field, onsite[0], link)
    plane = SLAB[:2]
    spread = call(
        pair_kernel,
        [(lax.axis_size(plane), *packed)],
        [SMEM, VMEM],
        place,
        lax.all_gather(tiles, "core"),
    )
    halves = lax.all_gather(jnp.sum(exchanged(spread, plane), axis=0), "core")
    scale = 1.0 / (orbitals * lax.axis_size(SLAB))
    correlation, projected = call(
        functools.partial(final_kernel, scale), [(columns, columns)] * 2, [VMEM], halves
    )
    return subspace[None], correlation, projected


def solution(mesh):
    torus = Mesh(mesh.devices.reshape(mesh.shape["quad"], 4, 4, 2), ("quad", *SLAB))
    return jax.shard_map(
        per_device,
        mesh=torus,
        in_specs=(
            P("quad", SLAB, None, None, None),
            P(SLAB, None, None),
            P(SLAB, None, None),
            P(SLAB, None, None),
            P("quad", None),
        ),
        out_specs=(P(SLAB, "quad", None), P(), P()),
        check_vma=False,
    )
```

```python
import functools

import jax
import jax.numpy as jnp
from jax import lax
from jax.experimental import pallas as pl
from jax.experimental.pallas import tpu as pltpu
from jax.sharding import Mesh
from jax.sharding import PartitionSpec as P

F32 = jnp.float32
BF16 = jnp.bfloat16
SLAB = ("y", "x", "core")
VMEM_BYTES = 24 << 20


def split(x):
    high = x.astype(BF16)
    return high, (x - high.astype(F32)).astype(BF16)


def dot(a, b):
    return jnp.dot(a, b, preferred_element_type=F32)


def times(left, right):
    return dot(left[0], right[0]) + (dot(left[0], right[1]) + dot(left[1], right[0]))


def wide(real, imag):
    return tuple(
        jnp.concatenate([jnp.concatenate([r, i], 1), jnp.concatenate([-i, r], 1)], 0)
        for r, i in zip(split(real), split(imag))
    )


class Run:
    def __init__(self, get, count, rows):
        self.get, self.count, self.rows = get, count, rows

    def part(self, half, block, k):
        return self.get(half, k)[block * self.rows : (block + 1) * self.rows, :]

    def state(self, half, which, k):
        return jnp.concatenate([self.part(half, 2 * which + p, k) for p in (0, 1)], 1)

    def wide(self, which, k):
        return wide(self.part(0, 2 * which, k), self.part(0, 2 * which + 1, k))

    def wide_c(self, k):
        return wide(self.part(0, 4, k), self.part(1, 4, k))


def merged(run, half):
    rows, last = run.rows, run.count - 1
    states = [run.state(half, 0, 0)]
    for k in range(1, run.count):
        state = times(split(states[-1]), run.wide(0, k))
        states.append(state + run.state(1, 0, k) if half else state)

    def from_left(k):
        term = times(split(states[k - 1]), run.wide(1, k))
        return term + run.state(1, 1, k) if half else term

    back = from_left(last)
    turn = jnp.concatenate([run.part(0, 4, last), run.part(1, 4, last)], 1)
    columns = back.shape[0]
    for k in range(last - 1, 0, -1):
        both = times(split(jnp.concatenate([back, turn], 0)), run.wide_c(k))
        back, turn = both[:columns] + from_left(k), both[columns:]
    first = run.wide_c(0)
    back = run.state(half, 1, 0) + times(split(back), first)
    at = slice(half * rows, (half + 1) * rows)
    turn = times(split(turn), (first[0][:, at], first[1][:, at]))
    ahead = states[-1]
    return ahead[:, :rows], ahead[:, rows:], back[:, :rows], back[:, rows:], turn


def entering(run, u, t):
    lefts, rights = [u], [t]
    for k in range(run.count - 1):
        b = run.state(1, 0, k)
        lefts.append(b if lefts[-1] is None else b + times(split(lefts[-1]), run.wide(0, k)))
    for k in range(run.count - 1, 0, -1):
        term = run.state(1, 1, k) + times(split(lefts[k]), run.wide(1, k))
        rights.append(term if rights[-1] is None else term + times(split(rights[-1]), run.wide_c(k)))
    return lefts, rights[::-1]


def chosen(options, index):
    result = options[0]
    for k, option in enumerate(options[1:], 1):
        result = jnp.where(index == k, option, result)
    return result


def gathered_run(own, other, half, rows):
    halves = (own, other) if half == 0 else (other, own)
    return Run(lambda h, k: halves[h].at[k], own.shape[0], rows)


def leaf_run(own, other, half, rows):
    sides = (own, other) if half == 0 else (other, own)
    return Run(lambda h, k: sides[k].at[h], 2, rows)


def leaf_kernel(factor, link, vectors, out, tops, bottoms, link_here, vectors_here, sems):
    rows, orbitals = link.shape[0], factor.shape[1]
    last = orbitals - rows
    copies = [
        pltpu.make_async_copy(link, link_here, sems.at[0]),
        pltpu.make_async_copy(vectors, vectors_here, sems.at[1]),
    ]
    for part in (0, 1):
        copies.append(
            pltpu.make_async_copy(factor.at[part, pl.ds(0, rows)], tops.at[part], sems.at[2 + part])
        )
        copies.append(
            pltpu.make_async_copy(factor.at[part, pl.ds(last, rows)], bottoms.at[part], sems.at[4 + part])
        )
    for copy in copies:
        copy.start()
    copies[0].wait()
    v, v_t = split(link_here[...]), split(link_here[...].T)
    copies[1].wait()
    y = vectors_here[...]
    for part in (0, 1):
        copies[2 + 2 * part].wait()
        copies[3 + 2 * part].wait()
        low, high = tops[part], bottoms[part]
        at = slice(part * rows, (part + 1) * rows)
        left = high[:, :rows]
        out[0, at, :] = (dot(v_t[0], left) + dot(v_t[1], left)).T
        out[1, at, :] = times(v_t, split(dot(high, y))).T
        at = slice((2 + part) * rows, (3 + part) * rows)
        out[0, at, :] = low[:, :rows].astype(F32).T
        out[1, at, :] = dot(low, y).T
        right = low[:, last:]
        out[part, 4 * rows :, :] = (dot(right, v[0]) + dot(right, v[1])).T


def merge_kernel(make, place, own, other, out):
    rows = out.shape[1] // 5
    for half in (0, 1):

        @pl.when(place[0] == half)
        def _():
            blocks = merged(make(own, other, half, rows), half)
            for k in range(out.shape[0]):
                for n, block in enumerate(blocks):
                    out[k, n * rows : (n + 1) * rows, :] = block


def base_kernel(weight, factor, vectors, out):
    y = vectors[...].astype(F32)
    real, imag = split(weight[0, 0] * y), split(-weight[0, 1] * y)
    out[...] = (dot(factor[0], real[0]) + dot(factor[0], real[1])) + (
        dot(factor[1], imag[0]) + dot(factor[1], imag[1])
    )


def halves_kernel(onsite, out):
    out[0], out[1] = split(0.5 * onsite[...])


def inner_kernel(place, leaf, leaf_2, rank, rank_2, out):
    rows = out.shape[0] // 10
    one = jnp.where(
        lax.broadcasted_iota(jnp.int32, (rows, rows), 0) == lax.broadcasted_iota(jnp.int32, (rows, rows), 1),
        1.0,
        0.0,
    )
    none = jnp.zeros((rows, rows), F32)
    unit, zero = jnp.concatenate([one, none], 1), jnp.zeros((rows, 2 * rows), F32)

    def stacked(*parts):
        return jnp.concatenate(parts, 0)

    def build(half):
        run = gathered_run(rank, rank_2, half, rows)
        last = run.count - 1
        lefts = [stacked(unit, zero), stacked(run.state(0, 0, 0), run.state(1, 0, 0))]
        for k in range(1, last):
            state = times(split(lefts[-1]), run.wide(0, k))
            lefts.append(state + stacked(zero, run.state(1, 0, k)))
        rights = [stacked(zero, zero, unit)]
        for k in range(last, 0, -1):
            term = times(split(lefts[k]), run.wide(1, k)) + stacked(zero, run.state(1, 1, k))
            turn = jnp.concatenate([run.part(0, 4, k), run.part(1, 4, k)], 1)
            if k == last:
                rights.append(stacked(term, turn))
            else:
                rights.append(times(split(rights[-1]), run.wide_c(k)) + stacked(term, zero))
        u, t = chosen(lefts, place[1]), chosen(rights[::-1], place[1])
        pair = leaf_run(leaf, leaf_2, half, rows)
        mid = times(split(u), pair.wide(0, 0)) + stacked(zero, pair.state(1, 0, 0))
        if half:
            u = mid
        else:
            term = times(split(mid), pair.wide(1, 1)) + stacked(zero, pair.state(1, 1, 1))
            t = times(split(t), pair.wide_c(1)) + stacked(term, zero)
        whole = stacked(u, t)
        for n in range(5):
            for p in (0, 1):
                at = (2 * n + p) * rows
                out[at : at + rows, :] = whole[n * rows : (n + 1) * rows, p * rows : (p + 1) * rows]

    for half in (0, 1):

        @pl.when(place[0] == half)
        def _():
            build(half)


def down_kernel(place, weight, factor, link, base, inner, file, file_2, out):
    rows, columns = link.shape
    orbitals = factor.shape[1]
    zero = jnp.zeros((columns, 2 * rows), F32)

    def block(n):
        return inner[2 * n * rows : (2 * n + 1) * rows, :], inner[(2 * n + 1) * rows : (2 * n + 2) * rows, :]

    def sweep(half):
        lefts, rights = entering(gathered_run(file, file_2, half, rows), None, None)
        u = split(chosen([zero] + lefts[1:], place[2]))
        t = split(chosen(rights[:-1] + [zero], place[2]))
        t = jnp.concatenate(block(3), 1) + (times(t, wide(*block(4))) + times(u, wide(*block(2))))
        u = jnp.concatenate(block(1), 1) + times(u, wide(*block(0)))
        w_re, w_im = weight[0, 0], weight[0, 1]
        turned, after = (
            ((w_re * x[:, :rows] - w_im * x[:, rows:]).T, (w_re * x[:, rows:] + w_im * x[:, :rows]).T)
            for x in (u, t)
        )
        v = split(link[...])
        total = base[...]
        for part, sign in ((0, 1.0), (1, -1.0)):
            f = factor[part]
            for field, cols in (
                (turned[part], slice(0, rows)),
                (times(v, split(after[part])), slice(orbitals - rows, orbitals)),
            ):
                high, low = split(sign * field)
                total = total + (dot(f[:, cols], high) + dot(f[:, cols], low))
        count = out.shape[0]
        share, spare = orbitals // count, rows // count
        for q in range(count):
            out[q, :share, :] = total[q * share : (q + 1) * share]
            out[q, share:, :] = after[0][q * spare : (q + 1) * spare]

    for half in (0, 1):

        @pl.when(place[0] == half)
        def _():
            sweep(half)


def sum_kernel(terms, spread, share_out):
    total = jnp.sum(terms[...], 0)
    for q in range(spread.shape[0]):
        spread[q] = total
    share_out[...] = total[: share_out.shape[0]]


def pair_kernel(place, both, spread):
    total = both[0, place[0]] + both[1, place[0]]
    for k in range(spread.shape[0]):
        spread[k] = total


def tile_kernel(field, onsite, link, out):
    columns = field.shape[2]
    orbitals, rows = onsite.shape[1], link.shape[0]
    share = orbitals // field.shape[0]
    whole = field[:, :share, :].reshape(orbitals, columns)
    following = field[:, share:, :].reshape(rows, columns)
    parts = split(whole)
    weighted = times((onsite[0], onsite[1]), parts)
    coupled = times(split(link[...]), split(following))
    weighted = jnp.concatenate([weighted[: orbitals - rows], weighted[orbitals - rows :] + coupled], 0)
    flipped = tuple(p.T for p in parts)
    gram = times(flipped, parts)
    tile = times(flipped, split(weighted))
    tile = tile + tile.T
    row = lax.broadcasted_iota(jnp.int32, gram.shape, 0)
    col = lax.broadcasted_iota(jnp.int32, gram.shape, 1)
    packed = jnp.where(row <= col, gram, tile)
    middle = jnp.sum(jnp.where(row == col, tile, 0.0), 0, keepdims=True)
    half = columns // 2
    for h in (0, 1):
        out[h, :half, :] = packed[h * half : (h + 1) * half]
        out[h, half:, :] = jnp.broadcast_to(middle, (8, columns))


def final_kernel(scale, halves, gram_out, tile_out):
    columns = gram_out.shape[1]
    half = columns // 2
    packed = jnp.concatenate([halves[0, :half, :], halves[1, :half, :]], 0) * scale
    middle = jnp.broadcast_to(halves[0, half : half + 1, :] * scale, packed.shape)
    flipped = packed.T
    row = lax.broadcasted_iota(jnp.int32, packed.shape, 0)
    col = lax.broadcasted_iota(jnp.int32, packed.shape, 1)
    gram_out[...] = jnp.where(row <= col, packed, flipped)
    tile_out[...] = jnp.where(row == col, middle, jnp.where(row > col, packed, flipped))


SMEM = pl.BlockSpec(memory_space=pltpu.SMEM)
VMEM = pl.BlockSpec(memory_space=pltpu.VMEM)
HBM = pl.BlockSpec(memory_space=pltpu.HBM)


def call(kernel, shapes, specs, *args, scratch=(), room=VMEM_BYTES, dtype=F32):
    shapes = [jax.ShapeDtypeStruct(s, dtype) for s in shapes]
    single = len(shapes) == 1
    return pl.pallas_call(
        kernel,
        out_shape=shapes[0] if single else shapes,
        in_specs=specs,
        out_specs=VMEM if single else [VMEM] * len(shapes),
        scratch_shapes=list(scratch),
        compiler_params=pltpu.CompilerParams(vmem_limit_bytes=room),
        cost_estimate=pl.CostEstimate(flops=1 << 26, bytes_accessed=1 << 20, transcendentals=0),
    )(*args)


def swapped(x):
    return lax.ppermute(x, "core", [(0, 1), (1, 0)])


def exchanged(x, axes):
    return lax.all_to_all(x, axes, 0, 0, tiled=True)


def per_device(factors, onsite, coupling, vectors, quad_weight):
    factor, link, here = factors[0, 0], coupling[0], vectors[0]
    orbitals, columns = here.shape
    rows = link.shape[0]
    quads = lax.axis_size("quad")
    place = jnp.stack([lax.axis_index(a) for a in ("core", "x", "y")]).astype(jnp.int32)
    half_map = (5 * rows, columns)

    leaf = call(
        leaf_kernel,
        [(2, *half_map)],
        [HBM] * 3,
        *(pltpu.with_memory_space_constraint(a, pltpu.HBM) for a in (factor, link, here)),
        scratch=[
            pltpu.VMEM((2, rows, orbitals), BF16),
            pltpu.VMEM((2, rows, orbitals), BF16),
            pltpu.VMEM(link.shape, F32),
            pltpu.VMEM(here.shape, BF16),
            pltpu.SemaphoreType.DMA((6,)),
        ],
    )
    base = call(base_kernel, [(orbitals, columns)], [SMEM, VMEM, VMEM], quad_weight, factor, here)
    onsite_parts = call(halves_kernel, [(2, orbitals, orbitals)], [VMEM], onsite[0], dtype=BF16)
    levels = [leaf, swapped(leaf)]
    for axis, make in (("x", leaf_run), ("y", gathered_run)):
        mine = call(
            functools.partial(merge_kernel, make),
            [(lax.axis_size(axis), *half_map)],
            [SMEM, VMEM, VMEM],
            place,
            *levels[-2:],
        )
        own = exchanged(mine, axis)
        levels += [own, swapped(own)]
        if axis == "x":
            levels[-1], base, onsite_parts = lax.optimization_barrier((levels[-1], base, onsite_parts))

    share = orbitals // quads
    rows_sent = share + rows // quads
    inner = call(inner_kernel, [(10 * rows, rows)], [SMEM] + [VMEM] * 4, place, *levels[:4])
    terms = call(
        down_kernel,
        [(quads, rows_sent, columns)],
        [SMEM, SMEM] + [VMEM] * 6,
        place,
        quad_weight,
        factor,
        link,
        base,
        inner,
        *levels[4:],
    )
    spread, subspace = call(
        sum_kernel,
        [(quads, rows_sent, columns), (share, columns)],
        [VMEM],
        exchanged(terms, "quad"),
    )
    field = exchanged(spread, "quad")
    packed = (columns // 2 + 8, columns)
    tiles = call(tile_kernel, [(2, *packed)], [VMEM] * 3, field, onsite_parts, link)
    plane = SLAB[:2]
    spread = call(
        pair_kernel,
        [(lax.axis_size(plane), *packed)],
        [SMEM, VMEM],
        place,
        lax.all_gather(tiles, "core"),
    )
    halves = lax.all_gather(jnp.sum(exchanged(spread, plane), axis=0), "core")
    scale = 1.0 / (orbitals * lax.axis_size(SLAB))
    correlation, projected = call(
        functools.partial(final_kernel, scale), [(columns, columns)] * 2, [VMEM], halves
    )
    return subspace[None], correlation, projected


def solution(mesh):
    torus = Mesh(mesh.devices.reshape(mesh.shape["quad"], 4, 4, 2), ("quad", *SLAB))
    return jax.shard_map(
        per_device,
        mesh=torus,
        in_specs=(
            P("quad", SLAB, None, None, None),
            P(SLAB, None, None),
            P(SLAB, None, None),
            P(SLAB, None, None),
            P("quad", None),
        ),
        out_specs=(P(SLAB, "quad", None), P(), P()),
        check_vma=False,
    )
```
